32 devices in a mesh: wide: 8 (over z, x), narrow: 4 (over y, core).
Axes of the slice: x: 2, y: 2, z: 4, core: 2. Of those that a mesh axis runs over, the one named last changes fastest.
Arguments:
- tokens: bfloat16 [4096, 1024], P(('wide', 'narrow')), may hold values from -6 to 6
- cotangent: bfloat16 [4096, 1024], P(('wide', 'narrow')), may hold values from -6 to 6
- lengths: int32 [32], P(('wide', 'narrow')), may hold values from 8 to 128, as said below
- gain_attn: bfloat16 [2, 1024], P(None, 'narrow'), may hold values from 0.5 to 1.5
- w_query: bfloat16 [2, 1024, 1024], P(None, 'narrow'), may hold values from -0.1875 to 0.1875
- w_key: bfloat16 [2, 1024, 1024], P(None, 'narrow'), may hold values from -0.1875 to 0.1875
- w_value: bfloat16 [2, 1024, 1024], P(None, 'narrow'), may hold values from -0.1875 to 0.1875
- w_out: bfloat16 [2, 1024, 1024], P(None, 'narrow'), may hold values from -0.75 to 0.75
- gain_mlp: bfloat16 [2, 1024], P(None, 'narrow'), may hold values from 0.5 to 1.5
- w_gate: bfloat16 [2, 1024, 2816], P(None, 'narrow'), may hold values from -0.1875 to 0.1875
- w_up: bfloat16 [2, 1024, 2816], P(None, 'narrow'), may hold values from -0.1875 to 0.1875
- w_down: bfloat16 [2, 2816, 1024], P(None, 'narrow'), may hold values from -0.109375 to 0.109375
Outputs:
- output: bfloat16 [4096, 1024], P(('wide', 'narrow'))
- grad_tokens: float32 [4096, 1024], P(('wide', 'narrow'))
- grad_gain_attn: float32 [2, 1024], P(None, 'narrow')
- grad_w_query: float32 [2, 1024, 1024], P(None, 'narrow')
- grad_w_key: float32 [2, 1024, 1024], P(None, 'narrow')
- grad_w_value: float32 [2, 1024, 1024], P(None, 'narrow')
- grad_w_out: float32 [2, 1024, 1024], P(None, 'narrow')
- grad_gain_mlp: float32 [2, 1024], P(None, 'narrow')
- grad_w_gate: float32 [2, 1024, 2816], P(None, 'narrow')
- grad_w_up: float32 [2, 1024, 2816], P(None, 'narrow')
- grad_w_down: float32 [2, 2816, 1024], P(None, 'narrow')
The draws below stay inside these ranges and needn't reach their ends.
Inputs may be any that keep to these rules, and one draw needn't show every extreme that they name: `lengths`: each slot's number of real tokens; positions at or beyond it are padding; in every draw one slot is full and one has the least length.
All inputs are finite; a program needn't handle non-finite values.
Results may differ from the reference program's by a relative error of at most 0.02.
Values may be sent and summed in bfloat16 or wider, within the bound.
A program may use at most 320 MiB of HBM per device.

```python
import math
import jax
import jax.numpy as jnp
from jax import lax

D = 1024
HEADS = 16
HEAD_DIM = 64
FF = 2816
SEQ = 128
LAYERS = 2
SLOTS = 32
TOKENS = 4096


def draw_lengths(key, part):
    least = max(1, SEQ // 16)
    first_key, second_key, third_key = jax.random.split(jax.random.fold_in(key, 7), 3)
    spread = jax.random.randint(first_key, (SLOTS,), 0, SEQ + 1)
    shaped = (spread * SEQ + spread * spread) // (2 * SEQ)
    drawn = least + shaped * (SEQ - least) // SEQ
    full_slot = jax.random.randint(second_key, (), 0, SLOTS)
    short_slot = (full_slot + 1 + jax.random.randint(third_key, (), 0, SLOTS - 1)) % SLOTS
    slot_ids = jnp.arange(SLOTS)
    drawn = jnp.where(slot_ids == full_slot, SEQ, drawn)
    drawn = jnp.where(slot_ids == short_slot, least, drawn)
    return drawn.astype(jnp.int32)


def level_of(key, shape, cuts, smallest, largest):
    def one(axis_at, blocks):
        steps = jax.random.uniform(jax.random.fold_in(jax.random.fold_in(key, 6), axis_at), (blocks,), jnp.float32, smallest / len(cuts), largest / len(cuts))
        return jnp.repeat(jnp.exp(steps), shape[axis_at] // blocks).reshape((-1,) + (1,) * (len(shape) - axis_at - 1))

    level = one(*cuts[0])
    for cut in cuts[1:]:
        level = level * one(*cut)
    return level


def normal_values(stream_key, extent, deviation, reach, shards=(), kind=jnp.bfloat16):
    factor_of = level_of(stream_key, extent, shards, -0.22, 0.18) if shards else 1.0
    result = jax.random.normal(stream_key, extent, jnp.float32) * deviation * factor_of
    return jnp.minimum(jnp.maximum(result, -reach), reach).astype(kind)


def setup_inputs(seed: int = 0) -> dict:
    key_list = jax.random.split(jax.random.key(seed), 13)
    return {
        "tokens": normal_values(key_list[0], (TOKENS, D), 1.0, 6.0, ((0, 32),)),
        "cotangent": normal_values(key_list[1], (TOKENS, D), 1.0, 6.0, ((0, 32),)),
        "lengths": draw_lengths(jax.random.fold_in(key_list[12], 71), 0),
        "gain_attn": jnp.clip(1.0 + 0.1 * jax.random.normal(key_list[3], (LAYERS, D), jnp.float32), 0.5, 1.5).astype(jnp.bfloat16),
        "w_query": normal_values(key_list[4], (LAYERS, D, D), D ** -0.5, 0.1875, ((1, 4),)),
        "w_key": normal_values(key_list[5], (LAYERS, D, D), D ** -0.5, 0.1875, ((1, 4),)),
        "w_value": normal_values(key_list[6], (LAYERS, D, D), D ** -0.5, 0.1875, ((1, 4),)),
        "w_out": normal_values(key_list[7], (LAYERS, D, D), (D // 16) ** -0.5, 0.75, ((1, 4),)),
        "gain_mlp": jnp.clip(1.0 + 0.1 * jax.random.normal(key_list[8], (LAYERS, D), jnp.float32), 0.5, 1.5).astype(jnp.bfloat16),
        "w_gate": normal_values(key_list[9], (LAYERS, D, FF), D ** -0.5, 0.1875, ((1, 4),)),
        "w_up": normal_values(key_list[10], (LAYERS, D, FF), D ** -0.5, 0.1875, ((1, 4),)),
        "w_down": normal_values(key_list[11], (LAYERS, FF, D), FF ** -0.5, 0.109375, ((1, 4),)),
    }


EPSILON = 1e-06
HIGHEST = lax.Precision.HIGHEST

@jax.custom_vjp
def low(v):
    return lax.optimization_barrier(v.astype(jnp.bfloat16)).astype(jnp.float32)

@jax.custom_vjp
def low_back(v):
    return v

def low_keep(v):
    return (low(v), None)

def low_pass(kept, grad):
    return (grad,)

def back_keep(v):
    return (v, None)

def back_low(kept, grad):
    return (low(grad),)
low.defvjp(low_keep, low_pass)
low_back.defvjp(back_keep, back_low)

def matmul(left, right):
    return jnp.dot(left, right, precision=HIGHEST)

def rms_scale(stream, gain):
    return stream * lax.rsqrt(lax.optimization_barrier(jnp.mean(stream * stream, axis=-1, keepdims=True)) + EPSILON) * gain

def rotary_tables():
    half_dim = HEAD_DIM // 2
    positions = jnp.arange(SEQ).astype(jnp.float32)
    frequency = jnp.exp(jnp.arange(half_dim).astype(jnp.float32) * (-2.0 * math.log(10000.0) / HEAD_DIM))
    angles = positions[:, None] * frequency[None, :]
    angles = jnp.concatenate([angles, angles], axis=1)
    return (jnp.cos(angles)[:, None, :], jnp.sin(angles)[:, None, :])

def rotate(tensor, cos_table, sin_table):
    half_dim = tensor.shape[-1] // 2
    turned = jnp.concatenate([-tensor[..., half_dim:], tensor[..., :half_dim]], axis=-1)
    return tensor * cos_table + turned * sin_table

def attention(query_rows, key_rows, value_rows, length):
    block_rows = min(512, SEQ)
    key_pos = jnp.arange(SEQ)

    def one_block(block_index):
        start_row = block_index * block_rows
        query_block = lax.dynamic_slice_in_dim(query_rows, start_row, block_rows, 0)
        scores = low_back(jnp.einsum('qhd,khd->hqk', query_block, key_rows, precision=HIGHEST) * HEAD_DIM ** (-0.5))
        query_pos = start_row + jnp.arange(block_rows)
        allowed = (key_pos[None, :] <= query_pos[:, None]) & (key_pos[None, :] < length)
        scores = jnp.where(allowed[None], scores, -1e+30)
        weights = jax.nn.softmax(scores, axis=-1)
        return jnp.einsum('hqk,khd->qhd', low(weights), value_rows, precision=HIGHEST)
    blocks = lax.map(jax.checkpoint(one_block), jnp.arange(SEQ // block_rows).astype(jnp.int32))
    return blocks.reshape(SEQ, HEADS * HEAD_DIM)

def run_layer(stream, weights, first_values, length, cos_table, sin_table):
    gain_attn, w_query, w_key, w_value, w_out, gain_mlp, w_gate, w_up, w_down = weights
    head_shape = (SEQ, HEADS, HEAD_DIM)
    normed = low(rms_scale(stream, gain_attn))
    query_rows = low(rotate(low_back(matmul(normed, w_query)).reshape(head_shape), cos_table, sin_table))
    key_rows = low(rotate(low_back(matmul(normed, w_key)).reshape(head_shape), cos_table, sin_table))
    value_rows = low_back(matmul(normed, w_value))
    if first_values is None:
        first_values = value_rows
        mixed_values = value_rows
    else:
        mixed_values = 0.5 * value_rows + 0.5 * first_values
    attended = low(low_back(attention(query_rows, key_rows, low(mixed_values).reshape(head_shape), length)))
    middle = stream + low_back(matmul(attended, w_out))
    normed_mid = low(rms_scale(middle, gain_mlp))
    gate_proj = low_back(matmul(normed_mid, w_gate))
    up_proj = low_back(matmul(normed_mid, w_up))
    hidden = low(jax.nn.silu(gate_proj) * up_proj)
    return (middle + low_back(matmul(hidden, w_down)), first_values)

def reference(tokens, cotangent, lengths, gain_attn, w_query, w_key, w_value, w_out, gain_mlp, w_gate, w_up, w_down):
    cos_table, sin_table = rotary_tables()
    weights = (gain_attn.astype(jnp.float32), w_query.astype(jnp.float32), w_key.astype(jnp.float32), w_value.astype(jnp.float32), w_out.astype(jnp.float32), gain_mlp.astype(jnp.float32), w_gate.astype(jnp.float32), w_up.astype(jnp.float32), w_down.astype(jnp.float32))
    inputs = tokens.astype(jnp.float32).reshape(SLOTS, SEQ, D)

    def forward(inputs, weights):

        def per_slot(carry_zero, slot_item):
            slot_in, length = slot_item
            first_weights = jax.tree.map(lambda stacked: stacked[0], weights)
            second_weights = jax.tree.map(lambda stacked: stacked[1], weights)
            stream, first_values = run_layer(slot_in, first_weights, None, length, cos_table, sin_table)
            stream, unused = run_layer(stream, second_weights, first_values, length, cos_table, sin_table)
            return (carry_zero, stream)
        carry_zero, outputs = lax.scan(jax.checkpoint(per_slot), jnp.zeros((), jnp.float32), (inputs, lengths))
        return outputs
    outputs, pullback = jax.vjp(forward, inputs, weights)
    valid_rows = (jnp.arange(SEQ)[None, :] < lengths[:, None]).astype(jnp.float32)
    seed_grad = cotangent.astype(jnp.float32).reshape(SLOTS, SEQ, D) * valid_rows[:, :, None]
    grad_inputs, grad_weights = pullback(seed_grad)
    return (outputs.reshape(TOKENS, D).astype(jnp.bfloat16), grad_inputs.reshape(TOKENS, D), grad_weights[0], grad_weights[1], grad_weights[2], grad_weights[3], grad_weights[4], grad_weights[5], grad_weights[6], grad_weights[7], grad_weights[8])
```

```python
import math

import jax
import jax.numpy as jnp
from jax import lax
from jax.sharding import PartitionSpec as P

HEADS = 16
HEAD_DIM = 64


EPSILON = 1e-06
NEG_FILL = -1e30


def matmul(left, right):
    return jnp.dot(left, right, preferred_element_type=jnp.float32)


def contract_rows(left, right):
    return lax.dot_general(
        left, right, (((0,), (0,)), ((), ())), preferred_element_type=jnp.float32
    )


def times_flip(left, right):
    return lax.dot_general(
        left, right, (((1,), (1,)), ((), ())), preferred_element_type=jnp.float32
    )


def rms_parts(stream, gain):
    inverse = lax.rsqrt(jnp.mean(stream * stream, axis=-1, keepdims=True) + EPSILON)
    return (stream * inverse * gain, inverse)


def rms_back(stream, inverse, gain, grad_normed):
    scaled = grad_normed * gain
    grad_gain = jnp.sum(grad_normed * stream * inverse, axis=0)
    grad_stream = inverse * scaled - stream * inverse * inverse * inverse * jnp.mean(
        scaled * stream, axis=-1, keepdims=True
    )
    return (grad_stream, grad_gain)


def rotary_tables(seq_len):
    half_dim = HEAD_DIM // 2
    positions = jnp.arange(seq_len).astype(jnp.float32)
    frequency = jnp.exp(
        jnp.arange(half_dim).astype(jnp.float32) * (-2.0 * math.log(10000.0) / HEAD_DIM)
    )
    angles = positions[:, None] * frequency[None, :]
    angles = jnp.concatenate([angles, angles], axis=1)
    return (jnp.cos(angles)[:, None, :], jnp.sin(angles)[:, None, :])


def rotate(tensor, cos_table, sin_table):
    half_dim = tensor.shape[-1] // 2
    turned = jnp.concatenate([-tensor[..., half_dim:], tensor[..., :half_dim]], axis=-1)
    return tensor * cos_table + turned * sin_table


def rotate_back(grad_rot, cos_table, sin_table):
    half_dim = grad_rot.shape[-1] // 2
    with_sine = grad_rot * sin_table
    turned = jnp.concatenate([with_sine[..., half_dim:], -with_sine[..., :half_dim]], axis=-1)
    return grad_rot * cos_table + turned


def block_mask(start_row, block_rows, seq_len, length):
    query_pos = start_row + jnp.arange(block_rows)
    key_pos = jnp.arange(seq_len)
    return (key_pos[None, :] <= query_pos[:, None]) & (key_pos[None, :] < length)


def attention_forward(query_rows, key_rows, value_rows, length):
    seq_len = query_rows.shape[0]
    block_rows = min(512, seq_len)
    scaling = HEAD_DIM ** (-0.5)

    def one_block(block_index):
        start_row = block_index * block_rows
        scores = (
            jnp.einsum("qhd,khd->hqk", query_rows, key_rows, preferred_element_type=jnp.float32)
            * scaling
        )
        scores = jnp.where(
            block_mask(start_row, block_rows, seq_len, length)[None], scores, NEG_FILL
        )
        highest = jnp.max(scores, axis=-1, keepdims=True)
        exponent = jnp.exp(scores - highest)
        totals = jnp.sum(exponent, axis=-1, keepdims=True)
        weights_low = (exponent / totals).astype(jnp.bfloat16)
        attended = jnp.einsum(
            "hqk,khd->qhd", weights_low, value_rows, preferred_element_type=jnp.float32
        )
        return (attended, (highest + jnp.log(totals))[..., 0])

    attended, log_totals = lax.map(one_block, jnp.arange(seq_len // block_rows))
    return (attended.reshape(seq_len, HEADS * HEAD_DIM), log_totals)


def attention_backward(query_rows, key_rows, value_rows, log_totals, grad_attended, length):
    seq_len = query_rows.shape[0]
    block_rows = min(512, seq_len)
    scaling = HEAD_DIM ** (-0.5)

    def one_block(carry_grads, block_index):
        grad_keys, grad_values = carry_grads
        start_row = block_index * block_rows
        scores = (
            jnp.einsum("qhd,khd->hqk", query_rows, key_rows, preferred_element_type=jnp.float32)
            * scaling
        )
        scores = jnp.where(
            block_mask(start_row, block_rows, seq_len, length)[None], scores, NEG_FILL
        )
        weights_now = jnp.exp(scores - log_totals[block_index][:, :, None])
        grad_weights = jnp.einsum(
            "qhd,khd->hqk", grad_attended, value_rows, preferred_element_type=jnp.float32
        )
        grad_values = grad_values + jnp.einsum(
            "hqk,qhd->khd",
            weights_now.astype(jnp.bfloat16),
            grad_attended,
            preferred_element_type=jnp.float32,
        )
        inner_sum = jnp.sum(weights_now * grad_weights, axis=-1, keepdims=True)
        grad_scores = (weights_now * (grad_weights - inner_sum)).astype(jnp.bfloat16)
        grad_query = (
            jnp.einsum("hqk,khd->qhd", grad_scores, key_rows, preferred_element_type=jnp.float32)
            * scaling
        )
        grad_keys = (
            grad_keys
            + jnp.einsum(
                "hqk,qhd->khd", grad_scores, query_rows, preferred_element_type=jnp.float32
            )
            * scaling
        )
        return ((grad_keys, grad_values), grad_query)

    zero_grads = jnp.zeros(key_rows.shape, jnp.float32)
    (grad_keys, grad_values), grad_queries = lax.scan(
        one_block, (zero_grads, zero_grads), jnp.arange(seq_len // block_rows)
    )
    return (grad_queries.reshape(query_rows.shape), grad_keys, grad_values)


def layer_forward(stream, weights, first_values, length, cos_table, sin_table):
    gain_attn, w_query, w_key, w_value, w_out, gain_mlp, w_gate, w_up, w_down = weights
    seq_len = stream.shape[0]
    head_shape = (seq_len, HEADS, HEAD_DIM)
    normed_full, inverse_attn = rms_parts(stream, gain_attn.astype(jnp.float32))
    normed = normed_full.astype(jnp.bfloat16)
    query_rows = rotate(matmul(normed, w_query).reshape(head_shape), cos_table, sin_table).astype(
        jnp.bfloat16
    )
    key_rows = rotate(matmul(normed, w_key).reshape(head_shape), cos_table, sin_table).astype(
        jnp.bfloat16
    )
    value_rows = matmul(normed, w_value)
    if first_values is None:
        mixed_values = value_rows
    else:
        mixed_values = 0.5 * value_rows + 0.5 * first_values
    mixed_low = mixed_values.astype(jnp.bfloat16).reshape(head_shape)
    attended, log_totals = attention_forward(query_rows, key_rows, mixed_low, length)
    attended_low = attended.astype(jnp.bfloat16)
    middle = stream + matmul(attended_low, w_out)
    normed_mid_full, inverse_mlp = rms_parts(middle, gain_mlp.astype(jnp.float32))
    normed_mid = normed_mid_full.astype(jnp.bfloat16)
    gate_proj = matmul(normed_mid, w_gate)
    up_proj = matmul(normed_mid, w_up)
    hidden = (jax.nn.silu(gate_proj) * up_proj).astype(jnp.bfloat16)
    result = middle + matmul(hidden, w_down)
    saved = (
        inverse_attn,
        normed,
        query_rows,
        key_rows,
        mixed_low,
        log_totals,
        attended_low,
        middle,
        inverse_mlp,
        normed_mid,
        gate_proj,
        up_proj,
        hidden,
    )
    return (result, value_rows, saved)


def layer_backward(
    stream, weights, first_values, values_extra, length, cos_table, sin_table, grad_result, saved
):
    gain_attn, w_query, w_key, w_value, w_out, gain_mlp, w_gate, w_up, w_down = weights
    (
        inverse_attn,
        normed,
        query_rows,
        key_rows,
        mixed_low,
        log_totals,
        attended_low,
        middle,
        inverse_mlp,
        normed_mid,
        gate_proj,
        up_proj,
        hidden,
    ) = saved
    seq_len = stream.shape[0]
    width = HEADS * HEAD_DIM
    head_shape = (seq_len, HEADS, HEAD_DIM)
    grad_result_low = grad_result.astype(jnp.bfloat16)
    grad_hidden = times_flip(grad_result_low, w_down)
    sigmoid_gate = jax.nn.sigmoid(gate_proj)
    grad_gate = (
        grad_hidden * up_proj * sigmoid_gate * (1.0 + gate_proj * (1.0 - sigmoid_gate))
    ).astype(jnp.bfloat16)
    grad_up = (grad_hidden * gate_proj * sigmoid_gate).astype(jnp.bfloat16)
    grad_normed_mid = times_flip(grad_gate, w_gate) + times_flip(grad_up, w_up)
    grad_middle, grad_gain_mlp = rms_back(
        middle, inverse_mlp, gain_mlp.astype(jnp.float32), grad_normed_mid
    )
    grad_middle = grad_middle + grad_result
    grad_middle_low = grad_middle.astype(jnp.bfloat16)
    grad_attended = times_flip(grad_middle_low, w_out).astype(jnp.bfloat16).reshape(head_shape)
    grad_query_rot, grad_key_rot, grad_mixed = attention_backward(
        query_rows, key_rows, mixed_low, log_totals, grad_attended, length
    )
    grad_query = (
        rotate_back(grad_query_rot, cos_table, sin_table)
        .reshape(seq_len, width)
        .astype(jnp.bfloat16)
    )
    grad_key = (
        rotate_back(grad_key_rot, cos_table, sin_table).reshape(seq_len, width).astype(jnp.bfloat16)
    )
    grad_mixed = grad_mixed.reshape(seq_len, width)
    if first_values is None:
        grad_value = (grad_mixed + values_extra).astype(jnp.bfloat16)
        extra_out = None
    else:
        grad_value = (0.5 * grad_mixed).astype(jnp.bfloat16)
        extra_out = 0.5 * grad_mixed
    grad_normed = (
        times_flip(grad_query, w_query)
        + times_flip(grad_key, w_key)
        + times_flip(grad_value, w_value)
    )
    grad_stream, grad_gain_attn = rms_back(
        stream, inverse_attn, gain_attn.astype(jnp.float32), grad_normed
    )
    grad_stream = grad_stream + grad_middle
    factors = (
        normed,
        attended_low,
        normed_mid,
        hidden,
        grad_query,
        grad_key,
        grad_value,
        grad_middle_low,
        grad_gate,
        grad_up,
        grad_result_low,
    )
    return (grad_stream, factors, (grad_gain_attn, grad_gain_mlp), extra_out)


def fetch_layer(params, layer_index):
    return tuple(
        lax.all_gather(param[layer_index], "narrow", axis=0, tiled=True) for param in params
    )


def share_columns(rows):
    return lax.all_to_all(rows, "narrow", split_axis=1, concat_axis=0, tiled=True)


def shard_grads(factors):
    normed, attended, normed_mid, hidden = (share_columns(rows) for rows in factors[:4])
    full = lax.all_gather(jnp.concatenate(factors[4:], axis=1), "narrow", axis=0, tiled=True)
    width = HEADS * HEAD_DIM
    inner = factors[8].shape[1]
    cuts = [0]
    for size in (3 * width, width, 2 * inner, width):
        cuts.append(cuts[-1] + size)
    parts = [full[:, a:b] for a, b in zip(cuts[:-1], cuts[1:])]
    upper = jnp.concatenate(
        [
            contract_rows(normed, parts[0]).astype(jnp.bfloat16),
            contract_rows(attended, parts[1]).astype(jnp.bfloat16),
            contract_rows(normed_mid, parts[2]).astype(jnp.bfloat16),
        ],
        axis=1,
    )
    lower = contract_rows(hidden, parts[3]).astype(jnp.bfloat16)
    return (upper, lower)


def spread_grads(upper, lower, gain_grads, inner):
    width = HEADS * HEAD_DIM
    upper, lower = lax.psum((upper, lower), "wide")
    gains = lax.psum_scatter(
        jnp.stack(gain_grads), "narrow", scatter_dimension=1, tiled=True
    )
    gains = lax.psum(gains, "wide")
    cuts = [0]
    for size in (width, width, width, width, inner, inner):
        cuts.append(cuts[-1] + size)
    query, key, value, out, gate, up = (
        upper[:, a:b].astype(jnp.float32) for a, b in zip(cuts[:-1], cuts[1:])
    )
    return (gains[0], query, key, value, out, gains[1], gate, up, lower.astype(jnp.float32))


def shards(
    tokens,
    cotangent,
    lengths,
    gain_attn,
    w_query,
    w_key,
    w_value,
    w_out,
    gain_mlp,
    w_gate,
    w_up,
    w_down,
):
    params = (gain_attn, w_query, w_key, w_value, w_out, gain_mlp, w_gate, w_up, w_down)
    seq_len = tokens.shape[0]
    length = lengths[0]
    inner = w_gate.shape[2]
    cos_table, sin_table = rotary_tables(seq_len)
    start_stream = tokens.astype(jnp.float32)
    first_weights = fetch_layer(params, 0)
    mid_stream, first_values, first_saved = layer_forward(
        start_stream, first_weights, None, length, cos_table, sin_table
    )
    second_weights = fetch_layer(params, 1)
    final_stream, unused_values, second_saved = layer_forward(
        mid_stream, second_weights, first_values, length, cos_table, sin_table
    )
    valid_rows = (jnp.arange(seq_len) < length).astype(jnp.float32)[:, None]
    grad_final = cotangent.astype(jnp.float32) * valid_rows
    grad_mid, factors_two, gains_two, values_extra = layer_backward(
        mid_stream,
        second_weights,
        first_values,
        None,
        length,
        cos_table,
        sin_table,
        grad_final,
        second_saved,
    )
    reduced_two = spread_grads(*shard_grads(factors_two), gains_two, inner)
    grad_start, factors_one, gains_one, unused_extra = layer_backward(
        start_stream,
        first_weights,
        None,
        values_extra,
        length,
        cos_table,
        sin_table,
        grad_mid,
        first_saved,
    )
    reduced_one = spread_grads(*shard_grads(factors_one), gains_one, inner)
    stacked = [
        jnp.stack([one_part, two_part]) for one_part, two_part in zip(reduced_one, reduced_two)
    ]
    return (final_stream.astype(jnp.bfloat16), grad_start, *stacked)


def solution(mesh):
    return jax.shard_map(
        shards,
        mesh=mesh,
        in_specs=(
            P(("wide", "narrow"), None),
            P(("wide", "narrow"), None),
            P(("wide", "narrow")),
            P(None, "narrow"),
            P(None, "narrow", None),
            P(None, "narrow", None),
            P(None, "narrow", None),
            P(None, "narrow", None),
            P(None, "narrow"),
            P(None, "narrow", None),
            P(None, "narrow", None),
            P(None, "narrow", None),
        ),
        out_specs=(
            P(("wide", "narrow"), None),
            P(("wide", "narrow"), None),
            P(None, "narrow"),
            P(None, "narrow", None),
            P(None, "narrow", None),
            P(None, "narrow", None),
            P(None, "narrow", None),
            P(None, "narrow"),
            P(None, "narrow", None),
            P(None, "narrow", None),
            P(None, "narrow", None),
        ),
        check_vma=False,
    )
```
